32 devices in a mesh: grp: 2 (over y), gx: 4 (over z), gy: 4 (over x, core).
Axes of the slice: x: 2, y: 2, z: 4, core: 2. Of those that a mesh axis runs over, the one named last changes fastest.
Arguments:
- slowness: float32 [32, 128, 128], P(('grp', 'gx')), parts along dimension 0, may hold values from 1 to 2
- buoyancy: float32 [32, 128, 128], P(('grp', 'gx')), parts along dimension 0, may hold values from 0.5 to 1
- saved_fields: bfloat16 [8, 8, 32, 128, 128], P('gy', None, ('grp', 'gx')), parts along dimension 2, may hold values from -6 to 6
- adj_states: float32 [8, 2, 32, 128, 128], P('gy', None, ('grp', 'gx')), parts along dimension 2, may hold values from -6 to 6
- residual_traces: bfloat16 [8, 6, 32, 128], P('gy', None, ('grp', 'gx')), parts along dimension 2, may hold values from -6 to 6
- receiver_depth: int32 [16], P(('grp', 'gy')), parts along dimension 0, may hold values from 1 to 63
- sample: float32 [32, 128, 128], P(('grp', 'gx'), 'gy'), parts along dimension 0, may hold values from -6 to 6
- noise_pred: bfloat16 [32, 128, 128], P(('grp', 'gx'), 'gy'), parts along dimension 0, may hold values from -6 to 6
Outputs:
- adj_last: float32 [8, 32, 128, 128], P('gy', ('grp', 'gx')), parts along dimension 1
- precond_grad: float32 [32, 128, 128], P(('grp', 'gx'), 'gy'), parts along dimension 0
- sample_next: float32 [32, 128, 128], P(('grp', 'gx'), 'gy'), parts along dimension 0
The draws below stay inside these ranges and needn't reach their ends.
There are 2 independent parts, one for each index of `grp`. The reference program is written for one: setup_inputs(seed, part) draws one part's arguments, and reference() takes and returns one part's arrays. A program takes and returns all parts, laid end to end along the dimension named above; each array names one. Nothing has to cross between parts.
All inputs are finite; a program needn't handle non-finite values.
Results may differ from the reference program's by a relative error of at most 0.0003.
Values may be sent and summed in bfloat16 or wider, within the bound.
No kernel may reach another device: no remote copies, remote signals or barrier semaphores. Data moves between devices by JAX's collectives and lax.ppermute only.
A program may use at most 64 MiB of HBM per device.

```python
import math
import jax
import jax.numpy as jnp
from jax import lax

NZ = 128
STEPS = 6
LEVELS = 8
NX = 16
NY = 128
SHOTS = 8


def set_ends(result, stream_key, low, top_value):
    index_at = [jax.random.randint(jax.random.fold_in(stream_key, axis), (), 0, length) for axis, length in enumerate(result.shape)]
    main_axis = result.shape.index(max(result.shape))
    neighbour = index_at[:main_axis] + [(index_at[main_axis] + 1) % result.shape[main_axis]] + index_at[main_axis + 1:]
    return result.at[tuple(index_at)].set(low).at[tuple(neighbour)].set(top_value)


def block_levels(stream_key, extent, split, least, top_value):
    factor_of = 1.0
    for dim, shards_of in split:
        heights = jax.random.uniform(jax.random.fold_in(jax.random.fold_in(stream_key, 6), dim), (shards_of,), jnp.float32, least / len(split), top_value / len(split))
        factor_of = factor_of * jnp.repeat(jnp.exp(heights), extent[dim] // shards_of).reshape((-1,) + (1,) * (len(extent) - 1 - dim))
    return factor_of


def noise(own_key, dims, scale, most, split=(), held_as=jnp.bfloat16):
    result = scale * jax.random.normal(own_key, dims, jnp.float32)
    if split:
        result = result * block_levels(own_key, dims, split, -0.22, 0.18)
    return jnp.clip(result, -most, most).astype(held_as)


def setup_inputs(seed: int = 0, part: int = 0) -> dict:
    key_list = jax.random.split(jax.random.key(seed), 9)
    part_splits = jax.random.split(jax.random.fold_in(key_list[8], part), 9)
    slowness = jnp.clip(jnp.exp(math.log(2.0) - 0.6931472 * jax.random.uniform(part_splits[0], (NX, NY, NZ), jnp.float32) ** block_levels(part_splits[0], (NX, NY, NZ), ((0, 4),), -0.2, 0.2)), 1.0, 2.0)
    buoyancy = jnp.clip(jnp.exp(math.log(1.0) - 0.6931472 * jax.random.uniform(part_splits[1], (NX, NY, NZ), jnp.float32) ** block_levels(part_splits[1], (NX, NY, NZ), ((0, 4),), -0.2, 0.2)), 0.5, 1.0)
    saved_fields = noise(part_splits[2], (SHOTS, LEVELS, NX, NY, NZ), 1.0, 6.0, ((0, 4), (2, 4)))
    adj_states = noise(part_splits[3], (SHOTS, 2, NX, NY, NZ), 1.0, 6.0, ((0, 4), (2, 4)), jnp.float32)
    residual_traces = noise(part_splits[4], (SHOTS, STEPS, NX, NY), 1.0, 6.0, ((0, 4), (2, 4)))
    receiver_depth = set_ends(jax.random.randint(part_splits[5], (SHOTS,), 1, NZ // 2), jax.random.fold_in(part_splits[5], 1), 1, (NZ // 2) - 1).astype(jnp.int32)
    sample = noise(part_splits[6], (NX, NY, NZ), 1.0, 6.0, ((0, 4), (1, 4)), jnp.float32)
    noise_pred = noise(part_splits[7], (NX, NY, NZ), 1.0, 6.0, ((0, 4), (1, 4)))
    return {"slowness": slowness, "buoyancy": buoyancy, "saved_fields": saved_fields, "adj_states": adj_states, "residual_traces": residual_traces, "receiver_depth": receiver_depth, "sample": sample, "noise_pred": noise_pred}


time_square = 0.2


def pad_axis(operand, dimension):
    widths = [(0, 0)] * operand.ndim
    widths[dimension] = (1, 1)
    return jnp.pad(operand, widths)


def div_flux(wave_field, buoy_ext):
    face_x = 0.5 * (buoy_ext[1:] + buoy_ext[:-1])
    flow_x = face_x * (wave_field[..., 1:, :, :] - wave_field[..., :-1, :, :])
    summed = flow_x[..., 1:, :, :] - flow_x[..., :-1, :, :]
    centre = wave_field[..., 1:-1, :, :]
    buoy_mid = buoy_ext[1:-1]
    wave_pad = pad_axis(centre, centre.ndim - 2)
    buoy_pad = pad_axis(buoy_mid, 1)
    face_y = 0.5 * (buoy_pad[:, 1:] + buoy_pad[:, :-1])
    flow_y = face_y * (wave_pad[..., 1:, :] - wave_pad[..., :-1, :])
    summed = summed + (flow_y[..., 1:, :] - flow_y[..., :-1, :])
    wave_pad = pad_axis(centre, centre.ndim - 1)
    buoy_pad = pad_axis(buoy_mid, 2)
    face_z = 0.5 * (buoy_pad[..., 1:] + buoy_pad[..., :-1])
    flow_z = face_z * (wave_pad[..., 1:] - wave_pad[..., :-1])
    summed = summed + (flow_z[..., 1:] - flow_z[..., :-1])
    return summed


def reference(slowness, buoyancy, saved_fields, adj_states, residual_traces, receiver_depth, sample, noise_pred):
    modulus = 1.0 / (buoyancy * slowness * slowness)
    buoy_ext = pad_axis(buoyancy, 0)
    depth_ids = jnp.arange(NZ, dtype=jnp.int32)

    def one_shot(imaging, inputs):
        saved_one, states, traces, depth_index = inputs
        depth_plane = (depth_ids == depth_index).astype(jnp.float32)
        previous = states[0]
        current = states[1]
        for step_index in range(STEPS):
            level_index = STEPS - step_index
            source = traces[step_index].astype(jnp.float32)[:, :, None] * depth_plane
            spread = div_flux(pad_axis(current, 0), buoy_ext)
            updated = 2.0 * current - previous + time_square * modulus * (spread + source)
            previous, current = current, updated
            curvature = (saved_one[level_index + 1].astype(jnp.float32) - 2.0 * saved_one[level_index].astype(jnp.float32)
                         + saved_one[level_index - 1].astype(jnp.float32))
            imaging = imaging + updated * curvature
        return imaging, current

    imaging, adj_last = lax.scan(one_shot, jnp.zeros((NX, NY, NZ), jnp.float32),
                                 (saved_fields, adj_states, residual_traces, receiver_depth))
    gradient = 2.0 * imaging / (slowness * (STEPS * SHOTS))
    padded = jnp.pad(gradient, ((1, 1), (1, 1), (0, 0)))
    precond_grad = 0.5 * gradient + 0.125 * (padded[2:, 1:-1] + padded[:-2, 1:-1] + padded[1:-1, 2:] + padded[1:-1, :-2])
    sample_next = 1.02 * (sample - 0.2 * noise_pred.astype(jnp.float32)) - 0.5 * precond_grad
    return adj_last, precond_grad, sample_next
```

```python
import jax
import jax.numpy as jnp
from jax import lax
from jax.sharding import PartitionSpec as P

time_square = 0.2
WIRE = jnp.float16


def pad_axis(operand, dimension):
    widths = [(0, 0)] * operand.ndim
    widths[dimension] = (1, 1)
    return jnp.pad(operand, widths)


def div_flux(wave_field, buoy_ext):
    face_x = 0.5 * (buoy_ext[1:] + buoy_ext[:-1])
    flow_x = face_x * (wave_field[..., 1:, :, :] - wave_field[..., :-1, :, :])
    summed = flow_x[..., 1:, :, :] - flow_x[..., :-1, :, :]
    centre = wave_field[..., 1:-1, :, :]
    buoy_mid = buoy_ext[1:-1]
    wave_pad = pad_axis(centre, centre.ndim - 2)
    buoy_pad = pad_axis(buoy_mid, 1)
    face_y = 0.5 * (buoy_pad[:, 1:] + buoy_pad[:, :-1])
    flow_y = face_y * (wave_pad[..., 1:, :] - wave_pad[..., :-1, :])
    summed = summed + (flow_y[..., 1:, :] - flow_y[..., :-1, :])
    wave_pad = pad_axis(centre, centre.ndim - 1)
    buoy_pad = pad_axis(buoy_mid, 2)
    face_z = 0.5 * (buoy_pad[..., 1:] + buoy_pad[..., :-1])
    flow_z = face_z * (wave_pad[..., 1:] - wave_pad[..., :-1])
    summed = summed + (flow_z[..., 1:] - flow_z[..., :-1])
    return summed


def curvature_at(saved_fields, level_index):
    return (
        saved_fields[:, level_index + 1].astype(jnp.float32)
        - 2.0 * saved_fields[:, level_index].astype(jnp.float32)
        + saved_fields[:, level_index - 1].astype(jnp.float32)
    )


def field_bounds(steps_count):
    bounds = [6.0, 6.0]
    for _ in range(steps_count):
        bounds.append(2.0 * bounds[-1] + bounds[-2] + time_square * 2.0 * 6.0)
    return bounds[1:]


def wire_scale(bound):
    scale = 1.0
    while scale * 2.0 * bound < 65000.0:
        scale = scale * 2.0
    return scale


def on_device(
    slowness,
    buoyancy,
    saved_fields,
    adj_states,
    residual_traces,
    receiver_depth,
    sample,
    noise_pred,
):
    gx_count = lax.axis_size("gx")
    gy_count = lax.axis_size("gy")
    pair_count = gy_count // 2
    gx_index = lax.axis_index("gx")
    gy_index = lax.axis_index("gy")
    side = gy_index % 2
    pair = gy_index // 2
    lower = side == 0
    shots, _, layers, rows, depth_count = adj_states.shape
    own = layers // 2
    steps_count = residual_traces.shape[1]
    has_outer = jnp.where(lower, gx_index > 0, gx_index < gx_count - 1)

    outer_perm = []
    for z in range(gx_count - 1):
        for p in range(pair_count):
            a = z * gy_count + 2 * p + 1
            b = (z + 1) * gy_count + 2 * p
            outer_perm += [(a, b), (b, a)]
    inner_perm = [(g, g ^ 1) for g in range(gy_count)]

    def to_outer(v):
        return lax.ppermute(v, ("gx", "gy"), outer_perm)

    def to_inner(v):
        return lax.ppermute(v, "gy", inner_perm)

    def orient(v, dim):
        return jnp.where(lower, v, jnp.flip(v, dim))

    def flat(v):
        return v.reshape(-1, depth_count)

    adj = orient(adj_states, 2)
    traces = orient(residual_traces, 2).astype(jnp.float32)
    saved = orient(saved_fields, 2)
    slow = orient(slowness, 0)
    buoy = orient(buoyancy, 0)

    depth_row = jnp.broadcast_to(
        receiver_depth.astype(jnp.float32)[:, None], (shots, depth_count)
    )
    theirs = jnp.flip(adj[:, :, own:], 2)
    swap = jnp.concatenate([flat(theirs), flat(jnp.flip(traces, 2)), depth_row], axis=0)
    swap_in = to_inner(swap)

    scale0 = wire_scale(6.0)
    first_steps = list(range(0, steps_count, 2))

    def field_payload(states, trace):
        return jnp.concatenate(
            [
                flat(states[:, 1, :own]),
                flat(states[:, 0, :1]),
                flat(jnp.stack([trace[:, k, 0] for k in first_steps], 1)),
            ],
            axis=0,
        )

    payload1 = jnp.concatenate(
        [
            field_payload(adj, traces) * scale0,
            flat((buoy[:2] - 0.75) * scale0),
            flat((slow[:1] - 1.5) * scale0),
        ],
        axis=0,
    ).astype(WIRE)
    outer1 = to_outer(payload1)
    rim = jnp.concatenate([flat(adj[:, 1, :own]), flat(adj[:, 0, own - 1 : own])], axis=0)
    rim_in = to_inner(rim)
    saved_in = to_inner(jnp.flip(saved[:, :, own:], 2))

    n_adj = shots * 2 * own * rows
    adj_in = swap_in[:n_adj].reshape(shots, 2, own, rows, depth_count)
    n_tr = shots * steps_count * layers
    traces_in = swap_in[n_adj : n_adj + n_tr].reshape(shots, steps_count, layers, rows)
    depth_in = swap_in[n_adj + n_tr :]
    outer2 = to_outer((field_payload(adj_in, traces_in) * scale0).astype(WIRE))

    def split_outer(v):
        v = v.astype(jnp.float32) * (1.0 / scale0)
        a = shots * own * rows
        b = a + shots * rows
        c = b + shots * len(first_steps)
        return (
            v[:a].reshape(shots, own, rows, depth_count),
            v[a:b].reshape(shots, 1, rows, depth_count),
            v[b:c].reshape(shots, len(first_steps), rows),
            v[c:],
        )

    cur_o_b, prev_o_b, tr_o_b, coef = split_outer(outer1)
    cur_o_a, prev_o_a, tr_o_a, _ = split_outer(outer2)
    valid = has_outer.astype(jnp.float32)
    buoy_o = (coef[: own * rows].reshape(own, rows, depth_count) + 0.75) * valid
    slow_o = coef[own * rows :].reshape(1, rows, depth_count) + 1.5
    mod_o = valid / (jnp.maximum(buoy_o[:1], 0.5) * slow_o * slow_o)
    buoy_wide = jnp.concatenate([jnp.flip(buoy_o, 0), buoy], axis=0)
    mod_own = 1.0 / (buoy[: own + 1] * slow[: own + 1] * slow[: own + 1])
    mod_wide = jnp.concatenate([mod_o, mod_own], axis=0)
    cur_outer = jnp.flip(jnp.concatenate([cur_o_a, cur_o_b], axis=0), 1)
    prev_outer = jnp.concatenate([prev_o_a, prev_o_b], axis=0)
    tr_outer = jnp.concatenate([tr_o_a, tr_o_b], axis=0)

    n_cur = shots * own * rows
    rim_cur = rim_in[:n_cur].reshape(shots, own, rows, depth_count)
    rim_prev = rim_in[n_cur:].reshape(shots, 1, rows, depth_count)
    cur_inner = jnp.concatenate([adj[:, 1, own:], jnp.flip(rim_cur, 1)], axis=0)
    prev_inner = jnp.concatenate([adj[:, 0, own : own + 1], rim_prev], axis=0)
    current = jnp.concatenate([adj[:, 1, :own], adj_in[:, 1]], axis=0)
    previous = jnp.concatenate([adj[:, 0, :own], adj_in[:, 0]], axis=0)
    prev_rimmed = jnp.concatenate([prev_outer, previous, prev_inner], axis=1)
    traces_own = jnp.concatenate([traces, traces_in], axis=0)
    depth_ids = lax.broadcasted_iota(jnp.int32, (2 * shots, depth_count), 1)
    depth_row = jnp.concatenate([depth_row, depth_in], axis=0)
    depth_plane = (depth_ids.astype(jnp.float32) == depth_row).astype(jnp.float32)[:, None, None, :]
    saved_own = jnp.concatenate([saved[:, :, :own], saved_in], axis=0)

    def mirrored(v):
        return jnp.concatenate([v[shots:], v[:shots]], axis=0)

    imaging = jnp.zeros((own, rows, depth_count), jnp.float32)
    bounds = field_bounds(steps_count)
    for pair_index in range(steps_count // 2):
        first_step = 2 * pair_index
        if pair_index > 0:
            scale = wire_scale(bounds[first_step])
            out = mirrored(current)
            o_in = to_outer((out * scale).astype(WIRE))
            i_in = to_inner(out)
            cur_outer = jnp.flip(o_in.astype(jnp.float32) * (1.0 / scale), 1)
            cur_inner = jnp.flip(i_in, 1)
        curr_wide = jnp.concatenate([cur_outer, current, cur_inner], axis=1)
        trace_mid = jnp.concatenate(
            [tr_outer[:, pair_index][:, None], traces_own[:, first_step, : own + 1]], axis=1
        )
        source = trace_mid[..., None] * depth_plane
        middle = (
            2.0 * curr_wide[:, 1:-1]
            - prev_rimmed
            + time_square * mod_wide * (div_flux(curr_wide, buoy_wide) + source)
        )
        source = traces_own[:, first_step + 1, :own][..., None] * depth_plane
        updated = (
            2.0 * middle[:, 1:-1]
            - current
            + time_square * mod_own[:own] * (div_flux(middle, buoy_wide[1:-1]) + source)
        )
        imaging = imaging + jnp.sum(
            middle[:, 1:-1] * curvature_at(saved_own, steps_count - first_step), axis=0
        )
        imaging = imaging + jnp.sum(
            updated * curvature_at(saved_own, steps_count - first_step - 1), axis=0
        )
        prev_rimmed = middle
        current = updated

    back = to_inner(current[shots:])
    mine = current[:shots]
    adj_last = orient(jnp.concatenate([mine, jnp.flip(back, 1)], axis=1), 1)

    shots_total = shots * gy_count
    grad_part = 2.0 * imaging / (slow[:own] * (steps_count * shots_total))
    pair_rows = rows // pair_count
    padded = pad_axis(grad_part, 1)
    slices = [padded[:, q * pair_rows : (q + 1) * pair_rows + 2] for q in range(pair_count)]

    def slice_of(q):
        out = slices[0]
        for i in range(1, pair_count):
            out = jnp.where(q == i, slices[i], out)
        return out

    red = slice_of(pair)
    for d in range(1, pair_count):
        perm = [
            (2 * p + e, 2 * ((p + d) % pair_count) + e)
            for p in range(pair_count)
            for e in range(2)
        ]
        red = red + lax.ppermute(slice_of((pair + d) % pair_count), "gy", perm)
    far = to_outer(red[:1, 1:-1])
    near = to_inner(red[own - 1 : own, 1:-1])
    centre = red[:, 1:-1]
    tall = jnp.concatenate([far, centre, near], axis=0)
    precond = 0.5 * centre + 0.125 * (tall[2:] + tall[:-2] + red[:, 2:] + red[:, :-2])
    half = pair_rows // 2
    keep = jnp.where(lower, precond[:, :half], precond[:, half:])
    give = jnp.where(lower, precond[:, half:], precond[:, :half])
    got = to_inner(give)
    precond_grad = orient(jnp.concatenate([keep, jnp.flip(got, 0)], axis=0), 0)
    sample_next = 1.02 * (sample - 0.2 * noise_pred.astype(jnp.float32)) - 0.5 * precond_grad
    return (adj_last, precond_grad, sample_next)


def solution(mesh):
    return jax.shard_map(
        on_device,
        mesh=mesh,
        in_specs=(
            P(("grp", "gx"), None, None),
            P(("grp", "gx"), None, None),
            P("gy", None, ("grp", "gx"), None, None),
            P("gy", None, ("grp", "gx"), None, None),
            P("gy", None, ("grp", "gx"), None),
            P(("grp", "gy")),
            P(("grp", "gx"), "gy", None),
            P(("grp", "gx"), "gy", None),
        ),
        out_specs=(
            P("gy", ("grp", "gx"), None, None),
            P(("grp", "gx"), "gy", None),
            P(("grp", "gx"), "gy", None),
        ),
        check_vma=False,
    )
```

```python
import functools

import jax
import jax.numpy as jnp
from jax import lax
from jax.experimental import pallas as pl
from jax.experimental.pallas import tpu as pltpu
from jax.sharding import PartitionSpec as P

time_square = 0.2
WIRE = jnp.float16
F32 = jnp.float32
VMEM_LIMIT = 20 << 20
BLOCK = 16


def field_bounds(steps_count):
    bounds = [6.0, 6.0]
    for _ in range(steps_count):
        bounds.append(2.0 * bounds[-1] + bounds[-2] + time_square * 2.0 * 6.0)
    return bounds[1:]


def wire_scale(bound):
    scale = 1.0
    while scale * 2.0 * bound < 65000.0:
        scale = scale * 2.0
    return scale


def call(body, outs, *args, flops=1e6, name=None):
    spec = pl.BlockSpec(memory_space=pltpu.VMEM)
    return pl.pallas_call(
        body,
        out_shape=tuple(jax.ShapeDtypeStruct(s, F32) for s in outs),
        in_specs=[spec] * len(args),
        out_specs=(spec,) * len(outs),
        compiler_params=pltpu.CompilerParams(vmem_limit_bytes=VMEM_LIMIT),
        cost_estimate=pl.CostEstimate(flops=int(flops), bytes_accessed=4 << 20, transcendentals=0),
        name=name,
    )(*args)


def native(j, layers):
    return j + (lax.axis_index("gy") % 2) * (layers - 1 - 2 * j)


def spot(column, hot):
    return jnp.where(hot > 0.5, column, 0.0)


def payload_body(steps, scale, adj, buoy, slow, cols, hots, rows, out_a, out_b):
    shots, _, layers, ny, nz = adj.shape
    own = layers // 2
    for half, out in ((0, out_a), (1, out_b)):
        at = 0
        js = [0, 1] if half == 0 else [layers - 1, layers - 2]
        for s in range(shots):
            for j in js[:own]:
                out[at : at + ny, :] = adj[s, 1, native(j, layers)] * scale
                at += ny
        j = js[0]
        n = native(j, layers)
        mod = time_square / (buoy[n] * slow[n] * slow[n])
        for s in range(shots):
            c = (s * steps) * layers + j
            src = spot(cols[:, c : c + 1], hots[s : s + 1, :])
            out[at : at + ny, :] = (adj[s, 0, n] - mod * src) * scale
            at += ny
        if half == 0:
            for j in js:
                out[at : at + ny, :] = (buoy[native(j, layers)] - 0.75) * scale
                at += ny
            out[at : at + ny, :] = (slow[native(0, layers)] - 1.5) * scale
            at += ny
        out[at:, :] = rows[16 * half : 16 * half + 16, :] * scale


def prepare_body(
    steps, adj, adj_in, buoy, slow, wire_a, cols, hots, valid, cur, inner, co, cs, p_out, q_out
):
    shots, _, layers, ny, nz = adj.shape
    own = layers // 2
    both = 2 * shots
    for s in range(both):
        ref = adj if s < shots else adj_in
        w = (s + shots) % both
        for j in range(own):
            cur[s, j] = ref[s % shots, 1, native(j, layers)]
            inner[w, j] = ref[s % shots, 1, native(layers - 1 - j, layers)]
    base = 3 * shots * ny
    lane = lax.broadcasted_iota(jnp.int32, (BLOCK, nz), 1)
    left = lane > 0
    right = lane < nz - 1
    ok = valid[0:1, :]
    for y0 in range(0, ny, BLOCK):
        ys = slice(y0, y0 + BLOCK)
        b = []
        for d in (1, 0):
            b.append((wire_a[base + d * ny + y0 : base + d * ny + y0 + BLOCK, :] + 0.75) * ok)
        for j in range(own + 2):
            b.append(buoy[native(j, layers), ys, :])
        row = lax.broadcasted_iota(jnp.int32, (BLOCK, nz), 0) + y0
        for j in range(-1, own + 1):
            c = b[j + 2]
            if j < 0:
                sl = wire_a[base + 2 * ny + y0 : base + 2 * ny + y0 + BLOCK, :] + 1.5
                mod = ok * (time_square / (jnp.maximum(c, 0.5) * sl * sl))
                n = None
            else:
                n = native(j, layers)
                sl = slow[n, ys, :]
                mod = time_square / (c * sl * sl)
            if n is None:
                plane = lambda a, e: (wire_a[base + a : base + e, :] + 0.75) * ok
            else:
                plane = lambda a, e, n=n: buoy[n, a:e, :]
            if y0 > 0:
                above = plane(y0 - 1, y0 + BLOCK - 1)
            else:
                above = jnp.where(row > 0, pltpu.roll(c, 1, 0), 0.0)
            if y0 + BLOCK < ny:
                below = plane(y0 + 1, y0 + BLOCK + 1)
            else:
                below = jnp.where(row < ny - 1, pltpu.roll(c, BLOCK - 1, 0), 0.0)
            before = jnp.where(left, pltpu.roll(c, 1, 1), 0.0)
            after = jnp.where(right, pltpu.roll(c, nz - 1, 1), 0.0)
            faces = [
                0.5 * (b[j + 1] + c),
                0.5 * (b[j + 3] + c),
                0.5 * (above + c),
                0.5 * (below + c),
                0.5 * (before + c),
                0.5 * (after + c),
            ]
            total = sum(faces[1:], faces[0])
            co[j + 1, 0, ys, :] = 2.0 - mod * total
            faces[2] = jnp.where(row > 0, faces[2], 0.0)
            faces[3] = jnp.where(row < ny - 1, faces[3], 0.0)
            faces[4] = jnp.where(left, faces[4], 0.0)
            faces[5] = jnp.where(right, faces[5], 0.0)
            for i in range(6):
                co[j + 1, 1 + i, ys, :] = mod * faces[i]
            cs[j + 1, ys, :] = mod
            for s in range(both):
                ref = adj if s < shots else adj_in
                t = s % shots
                hot = hots[s : s + 1, :]
                if j >= 0:
                    k = (s * steps) * layers + j
                    p_out[s, j + 1, ys, :] = (
                        mod * spot(cols[ys, k : k + 1], hot) - ref[t, 0, n, ys, :]
                    )
                if 0 <= j < own:
                    k = (s * steps + 1) * layers + j
                    q_out[s, j, ys, :] = (
                        mod * spot(cols[ys, k : k + 1], hot) - ref[t, 1, n, ys, :]
                    )


def advance(co, j, fields, centre, extra, y0, ny, nz, total):
    ys = (y0, y0 + BLOCK)
    c = [co[j + 1, i, y0 : y0 + BLOCK, :] for i in range(7)]
    for s in range(total):
        u = fields(s, j, *ys)
        v = c[0] * u + extra(s, j)
        v = v + c[1] * fields(s, j - 1, *ys)
        v = v + c[2] * fields(s, j + 1, *ys)
        up = fields(s, j, y0 - 1, y0 + BLOCK - 1) if y0 > 0 else pltpu.roll(u, 1, 0)
        v = v + c[3] * up
        if y0 + BLOCK < ny:
            down = fields(s, j, y0 + 1, y0 + BLOCK + 1)
        else:
            down = pltpu.roll(u, BLOCK - 1, 0)
        v = v + c[4] * down
        v = v + c[5] * pltpu.roll(u, 1, 1)
        v = v + c[6] * pltpu.roll(u, nz - 1, 1)
        centre(s, j, v)


def chunk_body(first, shots, *refs):
    if first:
        co, cur, inner, p_in, q_in, wire_a, wire_b, mid, new = refs
    else:
        co, cur, inner, p_in, q_in, outer, mid, new = refs
    both, own, ny, nz = cur.shape

    def far(s, d, a, e):
        if not first:
            return outer[(s + shots) % both, d, a:e, :]
        ref = wire_b if s < shots else wire_a
        base = ((s % shots) * own + d) * ny
        return ref[base + a : base + e, :]

    def fields(s, j, a, e):
        if j < 0:
            return far(s, -1 - j, a, e)
        if j < own:
            return cur[s, j, a:e, :]
        return inner[(s + shots) % both, 2 * own - 1 - j, a:e, :]

    for y0 in range(0, ny, BLOCK):
        ys = slice(y0, y0 + BLOCK)

        def extra(s, j):
            if first and j < 0:
                ref = wire_b if s < shots else wire_a
                base = (shots * own + s % shots) * ny
                return -ref[base + y0 : base + y0 + BLOCK, :]
            return p_in[s, j + 1, ys, :]

        def put(s, j, v):
            mid[s, j + 1, ys, :] = v

        for j in range(-1, own + 1):
            advance(co, j, fields, put, extra, y0, ny, nz, both)

    def middle(s, j, a, e):
        return mid[s, j + 1, a:e, :]

    for y0 in range(0, ny, BLOCK):
        ys = slice(y0, y0 + BLOCK)

        def put(s, j, v):
            new[s, j, ys, :] = v

        for j in range(own):
            advance(co, j, middle, put, lambda s, j: q_in[s, j, ys, :], y0, ny, nz, both)


def image_body(steps, step, first, last, *refs):
    refs = list(refs)
    mid, new, saved, saved_in = refs[:4]
    del refs[:4]
    if not first:
        img_in = refs.pop(0)
    if last:
        slow, img = refs
    else:
        cols, hots, cs, outer_cols, img, p_out, q_out = refs
    both, own, ny, nz = new.shape
    shots, _, layers, _, _ = saved.shape
    level = steps - step
    for y0 in range(0, ny, BLOCK):
        ys = slice(y0, y0 + BLOCK)
        for j in range(own):
            n = native(j, layers)
            acc = None if first else img_in[j, ys, :]
            for s in range(both):
                ref = saved if s < shots else saved_in
                t = s % shots
                f = [ref[t, level + 1 - i, n, ys, :].astype(F32) for i in range(4)]
                term = mid[s, j + 1, ys, :] * (f[0] - 2.0 * f[1] + f[2])
                term = term + new[s, j, ys, :] * (f[1] - 2.0 * f[2] + f[3])
                acc = term if acc is None else acc + term
            if last:
                acc = acc / slow[n, ys, :]
            img[j, ys, :] = acc
        if last:
            continue
        for s in range(both):
            hot = hots[s : s + 1, :]
            for j in range(-1, own + 1):
                if j < 0:
                    k = s * (steps // 2) + (step + 2) // 2
                    col = outer_cols[ys, k : k + 1]
                else:
                    k = (s * steps + step + 2) * layers + j
                    col = cols[ys, k : k + 1]
                p_out[s, j + 1, ys, :] = cs[j + 1, ys, :] * spot(col, hot) - mid[s, j + 1, ys, :]
            for j in range(own):
                k = (s * steps + step + 3) * layers + j
                q_out[s, j, ys, :] = (
                    cs[j + 1, ys, :] * spot(cols[ys, k : k + 1], hot) - new[s, j, ys, :]
                )


def on_device(
    slowness,
    buoyancy,
    saved_fields,
    adj_states,
    residual_traces,
    receiver_depth,
    sample,
    noise_pred,
):
    gx_count = lax.axis_size("gx")
    gy_count = lax.axis_size("gy")
    pair_count = gy_count // 2
    gx_index = lax.axis_index("gx")
    gy_index = lax.axis_index("gy")
    lower = gy_index % 2 == 0
    pair = gy_index // 2
    shots, _, layers, ny, nz = adj_states.shape
    own = layers // 2
    both = 2 * shots
    steps = residual_traces.shape[1]
    has_outer = jnp.where(lower, gx_index > 0, gx_index < gx_count - 1)

    outer_perm = []
    across_perm = []
    for z in range(gx_count - 1):
        for p in range(pair_count):
            a = z * gy_count + 2 * p
            b = (z + 1) * gy_count + 2 * p
            outer_perm += [(a + 1, b), (b, a + 1)]
            across_perm += [(a, b), (b + 1, a + 1)]
    inner_perm = [(g, g ^ 1) for g in range(gy_count)]

    def to_outer(v):
        return lax.ppermute(v, ("gx", "gy"), outer_perm)

    def to_inner(v):
        return lax.ppermute(v, "gy", inner_perm)

    def orient(v, dim):
        return jnp.where(lower, v, jnp.flip(v, dim))

    scale0 = wire_scale(6.0 + time_square * 2.0 * 6.0)
    bounds = field_bounds(steps)

    adj_in = to_inner(adj_states)
    traces = orient(residual_traces, 2).astype(F32)
    lanes = lax.broadcasted_iota(jnp.int32, (shots, nz), 1)
    hot = (lanes == receiver_depth[:, None]).astype(F32)
    notes = jnp.concatenate([jnp.flip(traces, 2).reshape(-1, ny), hot], axis=0)
    notes_in = to_inner(notes)

    def columns(t):
        flat = t.reshape(-1, ny)
        return jnp.pad(flat, ((0, -flat.shape[0] % 128), (0, 0))).T

    rim_steps = list(range(0, steps, 2))

    def rim_rows(j):
        r = jnp.stack([traces[:, k, j] for k in rim_steps], 1).reshape(-1, ny)
        return jnp.pad(r, ((0, 16 - r.shape[0]), (0, 0)))

    rows = jnp.concatenate([rim_rows(0), rim_rows(layers - 1)], axis=0)
    size_a = (shots * own + shots + own + 1) * ny + 16
    size_b = (shots * own + shots) * ny + 16
    payload_a, payload_b = call(
        functools.partial(payload_body, steps, scale0),
        [(size_a, nz), (size_b, nz)],
        adj_states,
        buoyancy,
        slowness,
        columns(traces),
        hot,
        rows,
        name="payload",
    )
    got_a = to_outer(payload_a.astype(WIRE))
    got_b = lax.ppermute(payload_b.astype(WIRE), ("gx", "gy"), across_perm)
    saved_in = to_inner(saved_fields)
    wire_a = got_a.astype(F32) * (1.0 / scale0)
    wire_b = got_b.astype(F32) * (1.0 / scale0)

    n_tr = shots * steps * layers
    traces_in = notes_in[:n_tr].reshape(shots, steps, layers, ny)
    hots = jnp.concatenate([hot, notes_in[n_tr:]], axis=0)
    cols = columns(jnp.concatenate([traces, traces_in], axis=0))
    valid = jnp.broadcast_to(has_outer.astype(F32), (8, nz))
    half = (both, own, ny, nz)
    rim = (both, own + 2, ny, nz)
    cur, inner, co, cs, p_term, q_term = call(
        functools.partial(prepare_body, steps),
        [half, half, (own + 2, 7, ny, nz), (own + 2, ny, nz), rim, half],
        adj_states,
        adj_in,
        buoyancy,
        slowness,
        wire_a,
        cols,
        hots,
        valid,
        name="prepare",
    )
    n_rim = shots * len(rim_steps)
    outer_cols = columns(
        jnp.concatenate([wire_b[-16:][:n_rim], wire_a[-16:][:n_rim]], axis=0)
    )
    img = None
    for step in range(0, steps, 2):
        first = step == 0
        last = step + 2 >= steps
        if first:
            far = [wire_a, wire_b]
        else:
            scale = wire_scale(bounds[step])
            far = [to_outer((cur * scale).astype(WIRE)).astype(F32) * (1.0 / scale)]
            inner = to_inner(cur)
        if not first:
            tail = [] if img is None else [img]
            img, p_term, q_term = call(
                functools.partial(image_body, steps, step - 2, img is None, False),
                [(own, ny, nz), rim, half],
                mid,
                cur,
                saved_fields,
                saved_in,
                *tail,
                cols,
                hots,
                cs,
                outer_cols,
                name="image",
            )
        mid, cur = call(
            functools.partial(chunk_body, first, shots),
            [rim, half],
            co,
            cur,
            inner,
            p_term,
            q_term,
            *far,
            name="chunk",
        )
    back = to_inner(cur[shots:])
    shots_total = shots * gy_count
    (grad,) = call(
        functools.partial(image_body, steps, steps - 2, steps == 2, True),
        [(own, ny, nz)],
        mid,
        cur,
        saved_fields,
        saved_in,
        *([] if img is None else [img]),
        slowness,
        name="image",
    )
    grad = grad * (2.0 / (steps * shots_total))

    pair_rows = ny // pair_count
    padded = jnp.pad(grad, ((0, 0), (1, 1), (0, 0)))
    slices = [padded[:, q * pair_rows : (q + 1) * pair_rows + 2] for q in range(pair_count)]

    def slice_of(q):
        out = slices[0]
        for i in range(1, pair_count):
            out = jnp.where(q == i, slices[i], out)
        return out

    red = slice_of(pair)
    pieces = []
    for d in range(1, pair_count):
        perm = [
            (2 * p + e, 2 * ((p + d) % pair_count) + e)
            for p in range(pair_count)
            for e in range(2)
        ]
        pieces.append(lax.ppermute(slice_of((pair + d) % pair_count), "gy", perm))
    adj_last = orient(jnp.concatenate([cur[:shots], jnp.flip(back, 1)], axis=1), 1)
    pieces, adj_last = lax.optimization_barrier((pieces, adj_last))
    for piece in pieces:
        red = red + piece
    far = to_outer(red[:1, 1:-1])
    near = to_inner(red[own - 1 : own, 1:-1])
    centre = red[:, 1:-1]
    tall = jnp.concatenate([far, centre, near], axis=0)
    precond = 0.5 * centre + 0.125 * (tall[2:] + tall[:-2] + red[:, 2:] + red[:, :-2])
    part = pair_rows // 2
    keep = jnp.where(lower, precond[:, :part], precond[:, part:])
    give = jnp.where(lower, precond[:, part:], precond[:, :part])
    got = to_inner(give)
    precond_grad = orient(jnp.concatenate([keep, jnp.flip(got, 0)], axis=0), 0)
    sample_next = 1.02 * (sample - 0.2 * noise_pred.astype(F32)) - 0.5 * precond_grad
    return (adj_last, precond_grad, sample_next)


def solution(mesh):
    return jax.shard_map(
        on_device,
        mesh=mesh,
        in_specs=(
            P(("grp", "gx"), None, None),
            P(("grp", "gx"), None, None),
            P("gy", None, ("grp", "gx"), None, None),
            P("gy", None, ("grp", "gx"), None, None),
            P("gy", None, ("grp", "gx"), None),
            P(("grp", "gy")),
            P(("grp", "gx"), "gy", None),
            P(("grp", "gx"), "gy", None),
        ),
        out_specs=(
            P("gy", ("grp", "gx"), None, None),
            P(("grp", "gx"), "gy", None),
            P(("grp", "gx"), "gy", None),
        ),
        check_vma=False,
    )
```
